512 devices in a mesh: out: 16 (over y_hi, z), in: 32 (over y_lo, x, core).
Axes of the slice: x: 4, y: 8 (y_hi: 2, y_lo: 4; y = y_hi * 4 + y_lo), z: 8, core: 2. Of those that a mesh axis runs over, the one named last changes fastest.
Arguments:
- tensor: bfloat16 [1024, 1024, 1024], P('out', 'in'), may hold values from -0.01171875 to 0.01171875
- linear: bfloat16 [1024, 1024], P('out', 'in'), may hold values from -0.1875 to 0.1875
- adjoint_end: float32 [128, 1024], P(None, 'in'), may hold values from -6 to 6
- states: bfloat16 [2, 128, 1024], replicated, may hold values from -6 to 6
Outputs:
- adjoint_start: float32 [128, 1024], P(None, 'in')
The draws below stay inside these ranges and needn't reach their ends.
All inputs are finite; a program needn't handle non-finite values.
Results may differ from the reference program's by a relative error of at most 0.0045.
Values may be sent and summed in bfloat16 or wider, within the bound.
No kernel may reach another device: no remote copies, remote signals or barrier semaphores. Data moves between devices by JAX's collectives and lax.ppermute only.
A program may use at most 64 MiB of HBM per device.

```python
import jax
import jax.numpy as jnp
from jax import lax

M = 1024
TRAJ = 128
STEPS = 2


def strengthened(values, stream_key, source, target, shards_of, factor):
    owner, partner = [(jnp.arange(values.shape[dim]) // (values.shape[dim] // shards_of)).reshape([-1 if axis == dim else 1 for axis in range(values.ndim)]) for dim in (source, target)]
    chosen = jax.random.permutation(stream_key, shards_of)[partner]
    strong = (owner == chosen) | (owner == (partner + shards_of // 2) % shards_of)
    return jnp.where(strong, factor * values, values)


def level_of(stream_key, shape, shards, low, top_value):
    gain, own = 1.0, jax.random.fold_in(stream_key, 6)
    for position, shards_of in shards:
        heights = jnp.exp(jax.random.uniform(jax.random.fold_in(own, position), (shards_of,), jnp.float32, low / len(shards), top_value / len(shards)))
        gain = gain * jnp.repeat(heights, shape[position] // shards_of).reshape([-1 if axis == position else 1 for axis in range(len(shape))])
    return gain


def noise(own_key, extent, deviation, most, pieces=(), kind=jnp.bfloat16):
    factor_of = level_of(own_key, extent, pieces, -0.22, 0.18) if pieces else 1.0
    result = jax.random.normal(own_key, extent, jnp.float32) * deviation * factor_of
    return jnp.minimum(jnp.maximum(result, -most), most).astype(kind)


def gaussian_with(stream_key, extent, scale, most, shards, heavy, kind=jnp.bfloat16):
    values = scale * jax.random.normal(stream_key, extent, jnp.float32)
    if shards:
        values = values * level_of(stream_key, extent, shards, -0.22, 0.18)
    return jnp.clip(strengthened(values, jax.random.fold_in(stream_key, 3), *heavy), -most, most).astype(kind)


def setup_inputs(seed: int = 0) -> dict:
    key_of = jax.random.split(jax.random.key(seed), 5)
    tensor = gaussian_with(key_of[0], (M, M, M), (M * M) ** -0.5, 0.01171875, ((0, 16), (1, 32)), (1, 2, 32, 2.75))
    linear = noise(key_of[1], (M, M), M ** -0.5, 0.1875, ((0, 16), (1, 32)))
    adjoint_end = noise(key_of[2], (TRAJ, M), 1.0, 6.0, ((1, 32),), jnp.float32)
    states = noise(key_of[3], (STEPS, TRAJ, M), 1.0, 6.0)
    return dict(tensor=tensor, linear=linear, adjoint_end=adjoint_end, states=states)


step_size = 0.5


def reference(tensor, linear, adjoint_end, states):
    block = M // 16
    count = M // block
    adjoint = adjoint_end
    for number in range(STEPS - 1, -1, -1):
        state = states[number]
        low = adjoint.astype(jnp.bfloat16)

        def visit(carry, index):
            first, second = carry
            start = (index * block).astype(jnp.int32)
            piece = lax.dynamic_slice_in_dim(tensor, start, block, 0).reshape(block * M, M)
            lam_rows = lax.dynamic_slice_in_dim(low, start, block, 1)
            projected = lax.dot_general(state, piece, (((1,), (1,)), ((), ())), preferred_element_type=jnp.float32)
            projected = projected.reshape(TRAJ, block, M)
            first = first + jnp.einsum("bi,bij->bj", lam_rows.astype(jnp.float32), projected.astype(jnp.float32))
            pair = (lam_rows.astype(jnp.float32)[:, :, None] * state.astype(jnp.float32)[:, None, :]).astype(jnp.bfloat16)
            second = second + jnp.dot(pair.reshape(TRAJ, block * M), piece, preferred_element_type=jnp.float32)
            return (first, second), None

        zeros = jnp.zeros((TRAJ, M), jnp.float32)
        (first, second), _ = lax.scan(visit, (zeros, zeros), jnp.arange(count, dtype=jnp.int32))
        lin = jnp.dot(low, linear, preferred_element_type=jnp.float32)
        adjoint = adjoint + step_size * (lin + first + second)
    return adjoint
```

```python
import jax
import jax.numpy as jnp
import numpy as np
from jax import lax
from jax.sharding import Mesh, PartitionSpec as P

step_size = 0.5
AXES = ("yhi", "z", "ylo", "x", "core")
SIZES = (2, 8, 4, 4, 2)
OUT = ("yhi", "z")
IN = ("ylo", "x", "core")
CHIP = ("ylo", "x")


def ring(a, b, n):
    d = abs(a - b) % n
    return min(d, n - d)


def spread_pairs():
    pairs = []
    for o in range(16):
        yhi, z = divmod(o, 8)
        ylo, x = divmod(o, 4)
        hold = [(h, k) for h in range(2) for k in range(8)]
        want = [(a, b) for a in range(4) for b in range(4)]
        cost = np.array(
            [
                [ring(k, z, 8) + ring(h * 4 + ylo, yhi * 4 + a, 8) + ring(x, b, 4) for a, b in want]
                for h, k in hold
            ]
        )
        best = assign(cost)
        for i, j in enumerate(best):
            pairs.append(((hold[i][0] * 8 + hold[i][1]) * 16 + o, o * 16 + want[j][0] * 4 + want[j][1]))
    return pairs


def assign(cost):
    n = len(cost)
    for limit in range(int(cost.max()) + 1):
        owner = [-1] * n

        def place(i, seen):
            for j in range(n):
                if cost[i][j] <= limit and j not in seen:
                    seen.add(j)
                    if owner[j] < 0 or place(owner[j], seen):
                        owner[j] = i
                        return True
            return False

        if all(place(i, set()) for i in range(n)):
            match = [0] * n
            for j, i in enumerate(owner):
                match[i] = j
            return match
    raise ValueError("no matching")


def start_rows(own):
    perm = [(2 * a + c, 2 * b + c) for a, b in spread_pairs() for c in range(2)]
    return lax.ppermute(own, AXES, perm)


def core_half(partial):
    batch = partial.shape[1]
    both = lax.all_gather(partial.astype(jnp.bfloat16), "core")
    both = both.reshape(2, 16, 2, 32, batch)
    mine = lax.dynamic_index_in_dim(both, lax.axis_index("core"), 2, keepdims=False)
    return (mine[0].astype(jnp.float32) + mine[1].astype(jnp.float32)).astype(jnp.bfloat16)


def scatter_sum(pieces, axes):
    got = lax.all_to_all(pieces, axes, 0, 0, tiled=True)
    return jnp.sum(got.astype(jnp.float32), 0)


def spread_sum(piece, axes):
    copies = jnp.broadcast_to(piece.astype(jnp.bfloat16)[None], (16,) + piece.shape)
    got = lax.all_to_all(copies, axes, 0, 0, tiled=True)
    return jnp.sum(got.astype(jnp.float32), 0)


def partial_of(flat, linear, projected, cols, low, slot):
    rows, batch = low.shape
    width = cols.shape[0]
    low_float = low.astype(jnp.float32)
    pair = (low_float[:, None, :] * cols.astype(jnp.float32)[None]).astype(jnp.bfloat16)
    second = lax.dot_general(
        flat, pair.reshape(rows * width, batch), (((0,), (0,)), ((), ())), preferred_element_type=jnp.float32
    )
    first = jnp.sum(low_float[:, None, :] * projected.reshape(rows, width, batch), 0)
    lin = lax.dot_general(linear, low, (((0,), (0,)), ((), ())), preferred_element_type=jnp.float32)
    mine = lax.broadcasted_iota(jnp.int32, (1024 // width, 1, 1), 0) == slot
    return (second.reshape(-1, width, batch) + jnp.where(mine, (first + lin)[None], 0.0)).reshape(-1, batch)


def per_device(tensor, linear, adjoint_end, states):
    rows, width, modes = tensor.shape
    steps, batch = states.shape[:2]
    slot = lax.axis_index(IN)
    flat = tensor.reshape(rows * width, modes)
    own = adjoint_end.T
    lam = start_rows(own)
    projected = lax.dot_general(
        flat, states.reshape(steps * batch, modes), (((1,), (1,)), ((), ())), preferred_element_type=jnp.float32
    )
    total = None
    for number in range(steps - 1, -1, -1):
        low = lax.all_gather(lam.astype(jnp.bfloat16), "core").reshape(rows, batch)
        cols = lax.dynamic_slice_in_dim(states[number], slot * width, width, 1).T
        part = partial_of(
            flat, linear, projected[:, number * batch : (number + 1) * batch], cols, low, slot
        )
        total = part if total is None else total + part
        if number:
            lam = lam + step_size * spread_sum(scatter_sum(core_half(part), OUT), CHIP)
    last = spread_sum(scatter_sum(core_half(total), CHIP), OUT)
    return (own + step_size * last).T


def solution(mesh):
    fine = Mesh(mesh.devices.reshape(SIZES), AXES)
    placed = (P(OUT, IN, None), P(OUT, IN), P(None, IN), P())
    return jax.shard_map(
        per_device, mesh=fine, in_specs=placed, out_specs=P(None, IN), check_vma=False
    )
```

```python
import functools

import jax
import jax.numpy as jnp
import numpy as np
from jax import lax
from jax.experimental import pallas as pl
from jax.experimental.pallas import tpu as pltpu
from jax.sharding import Mesh, PartitionSpec as P

step_size = 0.5
VMEM = pl.BlockSpec(memory_space=pltpu.VMEM)
SMEM = pl.BlockSpec(memory_space=pltpu.SMEM)
LIMIT = 16 * 1024 * 1024
AXES = ("yhi", "z", "ylo", "x", "core")
SIZES = (2, 8, 4, 4, 2)
OUT = ("yhi", "z")
IN = ("ylo", "x", "core")
CHIP = ("ylo", "x")
PLANE = ("yhi", "ylo", "x")
R1 = "B"
R0 = "A"


def ring(a, b, n):
    d = abs(a - b) % n
    return min(d, n - d)


def spread_pairs():
    pairs = []
    for o in range(16):
        yhi, z = divmod(o, 8)
        ylo, x = divmod(o, 4)
        hold = [(h, k) for h in range(2) for k in range(8)]
        want = [(a, b) for a in range(4) for b in range(4)]
        cost = np.array(
            [
                [ring(k, z, 8) + ring(h * 4 + ylo, yhi * 4 + a, 8) + ring(x, b, 4) for a, b in want]
                for h, k in hold
            ]
        )
        best = assign(cost)
        for i, j in enumerate(best):
            pairs.append(((hold[i][0] * 8 + hold[i][1]) * 16 + o, o * 16 + want[j][0] * 4 + want[j][1]))
    return pairs


def assign(cost):
    n = len(cost)
    for limit in range(int(cost.max()) + 1):
        owner = [-1] * n

        def place(i, seen):
            for j in range(n):
                if cost[i][j] <= limit and j not in seen:
                    seen.add(j)
                    if owner[j] < 0 or place(owner[j], seen):
                        owner[j] = i
                        return True
            return False

        if all(place(i, set()) for i in range(n)):
            match = [0] * n
            for j, i in enumerate(owner):
                match[i] = j
            return match
    raise ValueError("no matching")


def start_rows(own):
    perm = [(2 * a + c, 2 * b + c) for a, b in spread_pairs() for c in range(2)]
    return lax.ppermute(own, AXES, perm)


def core_half(partial):
    both = lax.all_gather(partial, "core")
    mine = lax.dynamic_index_in_dim(both, lax.axis_index("core"), 1, keepdims=False)
    return (mine[0].astype(jnp.float32) + mine[1].astype(jnp.float32)).astype(jnp.bfloat16)


def exchange(pieces, axes):
    return lax.all_to_all(pieces, axes, 0, 0, tiled=True)


def total_of(got):
    return jnp.sum(got.astype(jnp.float32), 0)


def fold_kernel(got_ref, copies_ref):
    count, groups = got_ref.shape[:2]
    for g in range(groups):
        total = got_ref[0, g].astype(jnp.float32)
        for k in range(1, count):
            total = total + got_ref[k, g].astype(jnp.float32)
        total = total.astype(jnp.bfloat16)
        for m in range(copies_ref.shape[1]):
            copies_ref[g, m] = total


def fold(got, copies):
    groups, width, batch = got.shape[1:]
    out = pl.pallas_call(
        fold_kernel,
        out_shape=jax.ShapeDtypeStruct((groups, copies, width, batch), jnp.bfloat16),
        in_specs=[VMEM],
        out_specs=VMEM,
        compiler_params=pltpu.CompilerParams(vmem_limit_bytes=LIMIT),
        name="fold",
    )(got)
    return out.reshape(groups * copies, width, batch)


def to_out_blocks(half):
    if R1 == "A":
        return total_of(exchange(fold(exchange(half, OUT)[:, None], 16), CHIP))
    two = exchange(half.reshape((8, 2) + half.shape[1:]), "z")
    return total_of(exchange(fold(two, 16), PLANE))


def to_in_blocks(half):
    if R0 == "A":
        return total_of(exchange(fold(exchange(half, CHIP)[:, None], 16), OUT))
    both = jnp.broadcast_to(half[None], (2,) + half.shape).reshape((32,) + half.shape[1:])
    return total_of(exchange(fold(exchange(both, PLANE)[:, None], 8), "z"))


CHUNKS = 8

def load_kernel(slot_ref, tensor_ref, states_ref, kept_ref, projected_ref, cols_ref, sems):
    height = kept_ref.shape[0] // CHUNKS
    loads = []
    for c in range(CHUNKS):
        rows = pl.ds(c * height, height)
        loads.append(pltpu.make_async_copy(tensor_ref.at[rows], kept_ref.at[rows], sems.at[c]))
        loads[-1].start()
    states = states_ref[...]
    shape = (cols_ref.shape[0], states.shape[1])
    wanted = lax.broadcasted_iota(jnp.int32, shape, 0) + slot_ref[0] * shape[0]
    pick = (lax.broadcasted_iota(jnp.int32, shape, 1) == wanted).astype(jnp.bfloat16)
    along = (((1,), (1,)), ((), ()))
    cols_ref[...] = lax.dot_general(pick, states, along, preferred_element_type=jnp.float32)
    for c in range(CHUNKS):
        loads[c].wait()
        rows = slice(c * height, (c + 1) * height)
        projected_ref[rows, :] = lax.dot_general(
            kept_ref[rows, :], states, along, preferred_element_type=jnp.float32
        )


def load(flat, states, slot, width):
    height, modes = flat.shape
    count = states.shape[0]
    return pl.pallas_call(
        load_kernel,
        out_shape=(
            jax.ShapeDtypeStruct(flat.shape, flat.dtype),
            jax.ShapeDtypeStruct((height, count), jnp.float32),
            jax.ShapeDtypeStruct((width, count), jnp.float32),
        ),
        in_specs=[SMEM, pl.BlockSpec(memory_space=pl.ANY), VMEM],
        out_specs=(VMEM, VMEM, VMEM),
        scratch_shapes=[pltpu.SemaphoreType.DMA((CHUNKS,))],
        compiler_params=pltpu.CompilerParams(vmem_limit_bytes=LIMIT),
        name="load",
    )(slot, flat, states)


def step_kernel(has_prev, keep_total, number, order, *refs):
    slot_ref, low_ref, cols_ref, projected_ref, linear_ref, tensor_ref = refs[:6]
    refs = refs[6:]
    if has_prev:
        prev_ref, refs = refs[0], refs[1:]
    send_ref, refs = refs[0], refs[1:]
    if keep_total:
        total_ref, refs = refs[0], refs[1:]
    (pair_ref,) = refs
    rows, batch = low_ref.shape
    width = cols_ref.shape[0]
    mine = slice(number * batch, (number + 1) * batch)
    low = low_ref[...]
    low_float = low.astype(jnp.float32)
    cols = cols_ref[:, mine]
    first = jnp.dot(linear_ref[...], low, preferred_element_type=jnp.float32)
    some = 128 // width
    for c in range(rows // some):
        part = low_float[c * some : (c + 1) * some, :]
        spread = jnp.broadcast_to(part[:, None, :], (some, width, batch))
        here = slice(c * 128, (c + 1) * 128)
        pair = (spread * cols[None]).reshape(128, batch)
        pair_ref[:, here] = pair.T.astype(jnp.bfloat16)
        first = first + jnp.sum(spread * projected_ref[here, mine].reshape(some, width, batch), 0)
    slot = slot_ref[0]
    modes = tensor_ref.shape[1]
    each = 256
    pair = pair_ref[...]
    for n in range(modes // each):
        second = jnp.dot(
            pair, tensor_ref[:, n * each : (n + 1) * each], preferred_element_type=jnp.float32
        ).T
        for k in range(each // width):
            block, half = divmod(n * (each // width) + k, 2)
            piece = second[k * width : (k + 1) * width, :]
            piece = piece + jnp.where(slot == 2 * block + half, first, 0.0)
            if has_prev:
                piece = piece + prev_ref[half, block]
            if keep_total:
                total_ref[half, block] = piece
            send_ref[half, order[block]] = piece.astype(jnp.bfloat16)


def step(flat, linear_t, projected, number, cols, low, slot, prev, keep_total, order):
    modes = flat.shape[1]
    width, batch = cols.shape[0], low.shape[1]
    full = (2, modes // (2 * width), width, batch)
    args = [slot, low, cols, projected, linear_t, flat]
    if prev is not None:
        args.append(prev)
    shapes = [jax.ShapeDtypeStruct(full, jnp.bfloat16)]
    if keep_total:
        shapes.append(jax.ShapeDtypeStruct(full, jnp.float32))
    return pl.pallas_call(
        functools.partial(step_kernel, prev is not None, keep_total, number, tuple(order)),
        out_shape=shapes,
        in_specs=[SMEM] + [VMEM] * (len(args) - 1),
        out_specs=[VMEM] * len(shapes),
        scratch_shapes=[pltpu.VMEM((batch, flat.shape[0]), jnp.bfloat16)],
        compiler_params=pltpu.CompilerParams(vmem_limit_bytes=LIMIT),
        name="step",
    )(*args)


def per_device(tensor, linear, adjoint_end, states):
    rows, width, modes = tensor.shape
    steps, batch = states.shape[:2]
    slot = jnp.reshape(lax.axis_index(IN), (1,)).astype(jnp.int32)
    own = adjoint_end.T
    lam = start_rows(own)
    flat, projected, cols = load(
        tensor.reshape(rows * width, modes), states.reshape(steps * batch, modes), slot, width
    )
    order = range(16) if R1 == "A" else [b % 8 * 2 + b // 8 for b in range(16)]
    total = None
    for number in range(steps - 1, -1, -1):
        low = lax.all_gather(lam.astype(jnp.bfloat16), "core").reshape(rows, batch)
        send, *rest = step(
            flat, linear.T, projected, number, cols, low, slot, total, number > 0, order if number else range(16)
        )
        half = core_half(send)
        if number:
            total = rest[0]
            lam = lam + step_size * to_out_blocks(half)
    return (own + step_size * to_in_blocks(half)).T


def solution(mesh):
    fine = Mesh(mesh.devices.reshape(SIZES), AXES)
    placed = (P(OUT, IN, None), P(OUT, IN), P(None, IN), P())
    return jax.shard_map(
        per_device, mesh=fine, in_specs=placed, out_specs=P(None, IN), check_vma=False
    )
```

```python
import functools

import jax
import jax.numpy as jnp
import numpy as np
from jax import lax
from jax.experimental import pallas as pl
from jax.experimental.pallas import tpu as pltpu
from jax.sharding import Mesh, PartitionSpec as P

step_size = 0.5
VMEM = pl.BlockSpec(memory_space=pltpu.VMEM)
HBM = pl.BlockSpec(memory_space=pltpu.HBM)
SMEM = pl.BlockSpec(memory_space=pltpu.SMEM)
LIMIT = 16 * 1024 * 1024
AXES = ("yhi", "z", "ylo", "x", "core")
SIZES = (2, 8, 4, 4, 2)
OUT = ("yhi", "z")
IN = ("ylo", "x", "core")
CHIP = ("ylo", "x")
PLANE = ("yhi", "ylo", "x")
R1 = "B"
R0 = "A"


def ring(a, b, n):
    d = abs(a - b) % n
    return min(d, n - d)


def spread_pairs():
    pairs = []
    for o in range(16):
        yhi, z = divmod(o, 8)
        ylo, x = divmod(o, 4)
        hold = [(h, k) for h in range(2) for k in range(8)]
        want = [(a, b) for a in range(4) for b in range(4)]
        cost = np.array(
            [
                [ring(k, z, 8) + ring(h * 4 + ylo, yhi * 4 + a, 8) + ring(x, b, 4) for a, b in want]
                for h, k in hold
            ]
        )
        best = assign(cost)
        for i, j in enumerate(best):
            pairs.append(((hold[i][0] * 8 + hold[i][1]) * 16 + o, o * 16 + want[j][0] * 4 + want[j][1]))
    return pairs


def assign(cost):
    n = len(cost)
    for limit in range(int(cost.max()) + 1):
        owner = [-1] * n

        def place(i, seen):
            for j in sorted(range(n), key=lambda k: cost[i][k]):
                if cost[i][j] <= limit and j not in seen:
                    seen.add(j)
                    if owner[j] < 0 or place(owner[j], seen):
                        owner[j] = i
                        return True
            return False

        if all(place(i, set()) for i in range(n)):
            match = [0] * n
            for j, i in enumerate(owner):
                match[i] = j
            return match
    raise ValueError("no matching")


def start_rows(own):
    pairs = spread_pairs()
    same = [(2 * a + c, 2 * b + c) for a, b in pairs for c in range(2)]
    cross = [(2 * a + c, 2 * b + 1 - c) for a, b in pairs for c in range(2)]
    other = lax.ppermute(own.astype(jnp.bfloat16), AXES, cross)
    return lax.ppermute(own, AXES, same), other


def in_order(mine, other):
    first = lax.axis_index("core") == 0
    return jnp.concatenate([jnp.where(first, mine, other), jnp.where(first, other, mine)], 0)


def core_half(keep, send):
    both = lax.all_gather(send, "core")
    got = lax.dynamic_index_in_dim(both, 1 - lax.axis_index("core"), 0, keepdims=False)
    return (keep + got.astype(jnp.float32)).astype(jnp.bfloat16)


def exchange(pieces, axes):
    return lax.all_to_all(pieces, axes, 0, 0, tiled=True)


def total_of(got):
    return jnp.sum(got.astype(jnp.float32), 0)


def fold_kernel(got_ref, copies_ref):
    count, groups = got_ref.shape[:2]
    for g in range(groups):
        total = got_ref[0, g].astype(jnp.float32)
        for k in range(1, count):
            total = total + got_ref[k, g].astype(jnp.float32)
        total = total.astype(jnp.bfloat16)
        for m in range(copies_ref.shape[1]):
            copies_ref[g, m] = total


def fold(got, copies):
    groups, width, batch = got.shape[1:]
    out = pl.pallas_call(
        fold_kernel,
        out_shape=jax.ShapeDtypeStruct((groups, copies, width, batch), jnp.bfloat16),
        in_specs=[VMEM],
        out_specs=VMEM,
        compiler_params=pltpu.CompilerParams(vmem_limit_bytes=LIMIT),
        name="fold",
    )(got)
    return out.reshape(groups * copies, width, batch)


def to_out_blocks(half):
    if R1 == "A":
        return total_of(exchange(fold(exchange(half, OUT)[:, None], 16), CHIP))
    two = exchange(half.reshape((8, 2) + half.shape[1:]), "z")
    return total_of(exchange(fold(two, 16), PLANE))


def to_in_blocks(half):
    if R0 == "A":
        return total_of(exchange(fold(exchange(half, CHIP)[:, None], 16), OUT))
    both = jnp.broadcast_to(half[None], (2,) + half.shape).reshape((32,) + half.shape[1:])
    return total_of(exchange(fold(exchange(both, PLANE)[:, None], 8), "z"))


CHUNKS = 8

def load_kernel(slot_ref, tensor_ref, source_ref, kept_ref, projected_ref, cols_ref, states_ref, sems):
    height = kept_ref.shape[0] // CHUNKS
    first = pltpu.make_async_copy(source_ref, states_ref, sems.at[CHUNKS])
    first.start()
    loads = []
    for c in range(CHUNKS):
        rows = pl.ds(c * height, height)
        loads.append(pltpu.make_async_copy(tensor_ref.at[rows], kept_ref.at[rows], sems.at[c]))
        loads[-1].start()
    first.wait()
    states = states_ref[...]
    shape = (cols_ref.shape[0], states.shape[1])
    wanted = lax.broadcasted_iota(jnp.int32, shape, 0) + slot_ref[0] * shape[0]
    pick = (lax.broadcasted_iota(jnp.int32, shape, 1) == wanted).astype(jnp.bfloat16)
    along = (((1,), (1,)), ((), ()))
    cols_ref[...] = lax.dot_general(pick, states, along, preferred_element_type=jnp.float32)
    for c in range(CHUNKS):
        loads[c].wait()
        rows = slice(c * height, (c + 1) * height)
        projected_ref[rows, :] = lax.dot_general(
            kept_ref[rows, :], states, along, preferred_element_type=jnp.float32
        )


def load(flat, states, slot, width):
    height, modes = flat.shape
    count = states.shape[0]
    return pl.pallas_call(
        load_kernel,
        out_shape=(
            jax.ShapeDtypeStruct(flat.shape, flat.dtype),
            jax.ShapeDtypeStruct((height, count), jnp.float32),
            jax.ShapeDtypeStruct((width, count), jnp.float32),
        ),
        in_specs=[SMEM, HBM, HBM],
        out_specs=(VMEM, VMEM, VMEM),
        scratch_shapes=[pltpu.VMEM(states.shape, states.dtype), pltpu.SemaphoreType.DMA((CHUNKS + 1,))],
        compiler_params=pltpu.CompilerParams(vmem_limit_bytes=LIMIT),
        name="load",
    )(slot, flat, states)


def step_kernel(has_prev, keep_total, number, order, *refs):
    slot_ref, low_ref, cols_ref, projected_ref, linear_ref, tensor_ref = refs[:6]
    refs = refs[6:]
    if has_prev:
        prev_ref, refs = refs[0], refs[1:]
    keep_ref, send_ref, refs = refs[0], refs[1], refs[2:]
    if keep_total:
        total_ref, refs = refs[0], refs[1:]
    (pair_ref,) = refs
    rows, batch = low_ref.shape
    width = cols_ref.shape[0]
    mine = slice(number * batch, (number + 1) * batch)
    low = low_ref[...]
    low_float = low.astype(jnp.float32)
    cols = cols_ref[:, mine]
    first = jnp.dot(linear_ref[...], low, preferred_element_type=jnp.float32)
    some = 128 // width
    for c in range(rows // some):
        part = low_float[c * some : (c + 1) * some, :]
        spread = jnp.broadcast_to(part[:, None, :], (some, width, batch))
        here = slice(c * 128, (c + 1) * 128)
        pair = (spread * cols[None]).reshape(128, batch)
        pair_ref[:, here] = pair.T.astype(jnp.bfloat16)
        first = first + jnp.sum(spread * projected_ref[here, mine].reshape(some, width, batch), 0)
    slot = slot_ref[0]
    modes = tensor_ref.shape[1]
    each = 256
    pair = pair_ref[...]
    for n in range(modes // each):
        second = jnp.dot(
            pair, tensor_ref[:, n * each : (n + 1) * each], preferred_element_type=jnp.float32
        ).T
        for k in range(0, each // width, 2):
            block = (n * (each // width) + k) // 2
            halves = []
            for half in range(2):
                piece = second[(k + half) * width : (k + half + 1) * width, :]
                piece = piece + jnp.where(slot == 2 * block + half, first, 0.0)
                if has_prev:
                    piece = piece + prev_ref[half, block]
                if keep_total:
                    total_ref[half, block] = piece
                halves.append(piece)
            even = slot % 2 == 0
            keep_ref[order[block]] = jnp.where(even, halves[0], halves[1])
            send_ref[order[block]] = jnp.where(even, halves[1], halves[0]).astype(jnp.bfloat16)


def step(flat, linear_t, projected, number, cols, low, slot, prev, keep_total, order):
    modes = flat.shape[1]
    width, batch = cols.shape[0], low.shape[1]
    full = (2, modes // (2 * width), width, batch)
    args = [slot, low, cols, projected, linear_t, flat]
    if prev is not None:
        args.append(prev)
    shapes = [jax.ShapeDtypeStruct(full[1:], jnp.float32), jax.ShapeDtypeStruct(full[1:], jnp.bfloat16)]
    if keep_total:
        shapes.append(jax.ShapeDtypeStruct(full, jnp.float32))
    return pl.pallas_call(
        functools.partial(step_kernel, prev is not None, keep_total, number, tuple(order)),
        out_shape=shapes,
        in_specs=[SMEM] + [VMEM] * (len(args) - 1),
        out_specs=[VMEM] * len(shapes),
        scratch_shapes=[pltpu.VMEM((batch, flat.shape[0]), jnp.bfloat16)],
        compiler_params=pltpu.CompilerParams(vmem_limit_bytes=LIMIT),
        name="step",
    )(*args)


def per_device(tensor, linear, adjoint_end, states):
    rows, width, modes = tensor.shape
    steps, batch = states.shape[:2]
    slot = jnp.reshape(lax.axis_index(IN), (1,)).astype(jnp.int32)
    own = adjoint_end.T
    lam, other = start_rows(own)
    low = in_order(lam.astype(jnp.bfloat16), other)
    flat, projected, cols = load(
        tensor.reshape(rows * width, modes), states.reshape(steps * batch, modes), slot, width
    )
    order = range(16) if R1 == "A" else [b % 8 * 2 + b // 8 for b in range(16)]
    total = None
    for number in range(steps - 1, -1, -1):
        keep, send, *rest = step(
            flat, linear.T, projected, number, cols, low, slot, total, number > 0, order if number else range(16)
        )
        half = core_half(keep, send)
        if number:
            total = rest[0]
            lam = lam + step_size * to_out_blocks(half)
            low = lax.all_gather(lam.astype(jnp.bfloat16), "core").reshape(rows, batch)
    return (own + step_size * to_in_blocks(half)).T


def solution(mesh):
    fine = Mesh(mesh.devices.reshape(SIZES), AXES)
    placed = (P(OUT, IN, None), P(OUT, IN), P(None, IN), P())
    return jax.shard_map(
        per_device, mesh=fine, in_specs=placed, out_specs=P(None, IN), check_vma=False
    )
```

```python
import functools

import jax
import jax.numpy as jnp
import numpy as np
from jax import lax
from jax.experimental import pallas as pl
from jax.experimental.pallas import tpu as pltpu
from jax.sharding import Mesh, PartitionSpec as P

step_size = 0.5
VMEM = pl.BlockSpec(memory_space=pltpu.VMEM)
SMEM = pl.BlockSpec(memory_space=pltpu.SMEM)
LIMIT = 16 * 1024 * 1024
AXES = ("yhi", "z", "ylo", "x", "core")
SIZES = (2, 8, 4, 4, 2)
OUT = ("yhi", "z")
IN = ("ylo", "x", "core")
CHIP = ("x", "ylo")
PLANE = ("yhi", "ylo", "x")
R1 = "B"
R0 = "A"


def ring(a, b, n):
    d = abs(a - b) % n
    return min(d, n - d)


def spread_pairs():
    pairs = []
    for o in range(16):
        yhi, z = divmod(o, 8)
        ylo, x = divmod(o, 4)
        hold = [(h, k) for h in range(2) for k in range(8)]
        want = [(a, b) for a in range(4) for b in range(4)]
        cost = np.array(
            [
                [ring(k, z, 8) + ring(h * 4 + ylo, yhi * 4 + a, 8) + ring(x, b, 4) for a, b in want]
                for h, k in hold
            ]
        )
        best = assign(cost)
        for i, j in enumerate(best):
            pairs.append(((hold[i][0] * 8 + hold[i][1]) * 16 + o, o * 16 + want[j][0] * 4 + want[j][1]))
    return pairs


def assign(cost):
    n = len(cost)
    weight = cost.astype(np.int64) ** 4
    row_of = [-1] * n
    high, low = [0] * (n + 1), [0] * (n + 1)
    match = [n] * (n + 1)
    for i in range(n):
        match[n] = i
        col = n
        least = [1 << 60] * (n + 1)
        back = [n] * (n + 1)
        used = [False] * (n + 1)
        while match[col] != n:
            used[col] = True
            row, delta, nxt = match[col], 1 << 60, n
            for j in range(n):
                if not used[j]:
                    reduced = int(weight[row][j]) - high[row] - low[j]
                    if reduced < least[j]:
                        least[j], back[j] = reduced, col
                    if least[j] < delta:
                        delta, nxt = least[j], j
            for j in range(n + 1):
                if used[j]:
                    high[match[j]] += delta
                    low[j] -= delta
                else:
                    least[j] -= delta
            col = nxt
        while col != n:
            prev = back[col]
            match[col] = match[prev]
            col = prev
    for j in range(n):
        row_of[match[j]] = j
    return row_of


def start_rows(own):
    perm = [(2 * a + c, 2 * b + c) for a, b in spread_pairs() for c in range(2)]
    return lax.ppermute(own, AXES, perm)


def core_half(keep, send):
    both = lax.all_gather(send, "core")
    got = lax.dynamic_index_in_dim(both, 1 - lax.axis_index("core"), 0, keepdims=False)
    return (keep + got.astype(jnp.float32)).astype(jnp.bfloat16)


def exchange(pieces, axes):
    return lax.all_to_all(pieces, axes, 0, 0, tiled=True)


def total_of(got):
    return jnp.sum(got.astype(jnp.float32), 0)


def fold_kernel(got_ref, copies_ref):
    count, groups = got_ref.shape[:2]
    for g in range(groups):
        total = got_ref[0, g].astype(jnp.float32)
        for k in range(1, count):
            total = total + got_ref[k, g].astype(jnp.float32)
        total = total.astype(jnp.bfloat16)
        for m in range(copies_ref.shape[1]):
            copies_ref[g, m] = total


def fold(got, copies):
    groups, width, batch = got.shape[1:]
    out = pl.pallas_call(
        fold_kernel,
        out_shape=jax.ShapeDtypeStruct((groups, copies, width, batch), jnp.bfloat16),
        in_specs=[VMEM],
        out_specs=VMEM,
        compiler_params=pltpu.CompilerParams(vmem_limit_bytes=LIMIT),
        name="fold",
    )(got)
    return out.reshape(groups * copies, width, batch)


def to_out_blocks(half):
    if R1 == "A":
        return total_of(exchange(fold(exchange(half, OUT)[:, None], 16), CHIP))
    two = exchange(half.reshape((8, 2) + half.shape[1:]), "z")
    return total_of(exchange(fold(two, 16), PLANE))


def to_in_blocks(half):
    if R0 == "A":
        return total_of(exchange(fold(exchange(half, CHIP)[:, None], 16), OUT))
    both = jnp.broadcast_to(half[None], (2,) + half.shape).reshape((32,) + half.shape[1:])
    return total_of(exchange(fold(exchange(both, PLANE)[:, None], 8), "z"))


def load_kernel(slot_ref, tensor_ref, states_ref, projected_ref, cols_ref):
    states = states_ref[...]
    shape = (cols_ref.shape[0], states.shape[1])
    wanted = lax.broadcasted_iota(jnp.int32, shape, 0) + slot_ref[0] * shape[0]
    pick = (lax.broadcasted_iota(jnp.int32, shape, 1) == wanted).astype(jnp.bfloat16)
    along = (((1,), (1,)), ((), ()))
    cols_ref[...] = lax.dot_general(pick, states, along, preferred_element_type=jnp.float32)
    projected_ref[...] = lax.dot_general(
        tensor_ref[...], states, along, preferred_element_type=jnp.float32
    )


def load(flat, states, slot, width):
    height, modes = flat.shape
    count = states.shape[0]
    return pl.pallas_call(
        load_kernel,
        out_shape=(
            jax.ShapeDtypeStruct((height, count), jnp.float32),
            jax.ShapeDtypeStruct((width, count), jnp.float32),
        ),
        in_specs=[SMEM, VMEM, VMEM],
        out_specs=(VMEM, VMEM),
        compiler_params=pltpu.CompilerParams(vmem_limit_bytes=LIMIT),
        name="load",
    )(slot, flat, states)


def step_kernel(has_prev, keep_total, number, order, *refs):
    slot_ref, low_ref, cols_ref, projected_ref, linear_ref, tensor_ref = refs[:6]
    refs = refs[6:]
    if has_prev:
        prev_ref, refs = refs[0], refs[1:]
    keep_ref, send_ref, refs = refs[0], refs[1], refs[2:]
    if keep_total:
        total_ref, refs = refs[0], refs[1:]
    (pair_ref,) = refs
    rows, batch = low_ref.shape
    width = cols_ref.shape[0]
    mine = slice(number * batch, (number + 1) * batch)
    low = low_ref[...]
    low_float = low.astype(jnp.float32)
    cols = cols_ref[:, mine]
    first = jnp.dot(linear_ref[...], low, preferred_element_type=jnp.float32)
    some = 128 // width
    for c in range(rows // some):
        part = low_float[c * some : (c + 1) * some, :]
        spread = jnp.broadcast_to(part[:, None, :], (some, width, batch))
        here = slice(c * 128, (c + 1) * 128)
        pair = (spread * cols[None]).reshape(128, batch)
        pair_ref[:, here] = pair.T.astype(jnp.bfloat16)
        first = first + jnp.sum(spread * projected_ref[here, mine].reshape(some, width, batch), 0)
    slot = slot_ref[0]
    modes = tensor_ref.shape[1]
    each = 256
    pair = pair_ref[...]
    for n in range(modes // each):
        second = jnp.dot(
            pair, tensor_ref[:, n * each : (n + 1) * each], preferred_element_type=jnp.float32
        ).T
        for k in range(0, each // width, 2):
            block = (n * (each // width) + k) // 2
            halves = []
            for half in range(2):
                piece = second[(k + half) * width : (k + half + 1) * width, :]
                piece = piece + jnp.where(slot == 2 * block + half, first, 0.0)
                if has_prev:
                    piece = piece + prev_ref[half, block]
                if keep_total:
                    total_ref[half, block] = piece
                halves.append(piece)
            even = slot % 2 == 0
            keep_ref[order[block]] = jnp.where(even, halves[0], halves[1])
            send_ref[order[block]] = jnp.where(even, halves[1], halves[0]).astype(jnp.bfloat16)


def step(flat, linear_t, projected, number, cols, low, slot, prev, keep_total, order):
    modes = flat.shape[1]
    width, batch = cols.shape[0], low.shape[1]
    full = (2, modes // (2 * width), width, batch)
    args = [slot, low, cols, projected, linear_t, flat]
    if prev is not None:
        args.append(prev)
    shapes = [jax.ShapeDtypeStruct(full[1:], jnp.float32), jax.ShapeDtypeStruct(full[1:], jnp.bfloat16)]
    if keep_total:
        shapes.append(jax.ShapeDtypeStruct(full, jnp.float32))
    return pl.pallas_call(
        functools.partial(step_kernel, prev is not None, keep_total, number, tuple(order)),
        out_shape=shapes,
        in_specs=[SMEM] + [VMEM] * (len(args) - 1),
        out_specs=[VMEM] * len(shapes),
        scratch_shapes=[pltpu.VMEM((batch, flat.shape[0]), jnp.bfloat16)],
        compiler_params=pltpu.CompilerParams(vmem_limit_bytes=LIMIT),
        name="step",
    )(*args)


def per_device(tensor, linear, adjoint_end, states):
    rows, width, modes = tensor.shape
    steps, batch = states.shape[:2]
    slot = jnp.reshape(lax.axis_index(IN), (1,)).astype(jnp.int32)
    own = adjoint_end.T
    lam = start_rows(own)
    flat = tensor.reshape(rows * width, modes)
    projected, cols = load(flat, states.reshape(steps * batch, modes), slot, width)
    order = range(16) if R1 == "A" else [b % 8 * 2 + b // 8 for b in range(16)]
    last = [b % 4 * 4 + b // 4 for b in range(16)]
    total = None
    for number in range(steps - 1, -1, -1):
        low = lax.all_gather(lam.astype(jnp.bfloat16), "core").reshape(rows, batch)
        keep, send, *rest = step(
            flat, linear.T, projected, number, cols, low, slot, total, number > 0, order if number else last
        )
        half = core_half(keep, send)
        if number:
            total = rest[0]
            lam = lam + step_size * to_out_blocks(half)
    return (own + step_size * to_in_blocks(half)).T


def solution(mesh):
    fine = Mesh(mesh.devices.reshape(SIZES), AXES)
    placed = (P(OUT, IN, None), P(OUT, IN), P(None, IN), P())
    return jax.shard_map(
        per_device, mesh=fine, in_specs=placed, out_specs=P(None, IN), check_vma=False
    )
```

```python
import functools

import jax
import jax.numpy as jnp
import numpy as np
from jax import lax
from jax.experimental import pallas as pl
from jax.experimental.pallas import tpu as pltpu
from jax.sharding import Mesh, PartitionSpec as P

step_size = 0.5
VMEM = pl.BlockSpec(memory_space=pltpu.VMEM)
SMEM = pl.BlockSpec(memory_space=pltpu.SMEM)
LIMIT = 16 * 1024 * 1024
AXES = ("yhi", "z", "ylo", "x", "core")
SIZES = (2, 8, 4, 4, 2)
OUT = ("yhi", "z")
IN = ("ylo", "x", "core")
CHIP = ("x", "ylo")
PLANE = ("yhi", "ylo", "x")
R1 = "A"
R0 = "A"


def ring(a, b, n):
    d = abs(a - b) % n
    return min(d, n - d)


def spread_pairs():
    pairs = []
    for o in range(16):
        yhi, z = divmod(o, 8)
        ylo, x = divmod(o, 4)
        hold = [(h, k) for h in range(2) for k in range(8)]
        want = [(a, b) for a in range(4) for b in range(4)]
        cost = np.array(
            [
                [ring(k, z, 8) + ring(h * 4 + ylo, yhi * 4 + a, 8) + ring(x, b, 4) for a, b in want]
                for h, k in hold
            ]
        )
        best = assign(cost)
        for i, j in enumerate(best):
            pairs.append(((hold[i][0] * 8 + hold[i][1]) * 16 + o, o * 16 + want[j][0] * 4 + want[j][1]))
    return pairs


def assign(cost):
    n = len(cost)
    weight = cost.astype(np.int64) ** 4
    row_of = [-1] * n
    high, low = [0] * (n + 1), [0] * (n + 1)
    match = [n] * (n + 1)
    for i in range(n):
        match[n] = i
        col = n
        least = [1 << 60] * (n + 1)
        back = [n] * (n + 1)
        used = [False] * (n + 1)
        while match[col] != n:
            used[col] = True
            row, delta, nxt = match[col], 1 << 60, n
            for j in range(n):
                if not used[j]:
                    reduced = int(weight[row][j]) - high[row] - low[j]
                    if reduced < least[j]:
                        least[j], back[j] = reduced, col
                    if least[j] < delta:
                        delta, nxt = least[j], j
            for j in range(n + 1):
                if used[j]:
                    high[match[j]] += delta
                    low[j] -= delta
                else:
                    least[j] -= delta
            col = nxt
        while col != n:
            prev = back[col]
            match[col] = match[prev]
            col = prev
    for j in range(n):
        row_of[match[j]] = j
    return row_of


def start_rows(own):
    perm = [(2 * a + c, 2 * b + c) for a, b in spread_pairs() for c in range(2)]
    return lax.ppermute(own, AXES, perm)


def core_half(keep, send):
    both = lax.all_gather(send, "core")
    got = lax.dynamic_index_in_dim(both, 1 - lax.axis_index("core"), 0, keepdims=False)
    return (keep + got.astype(jnp.float32)).astype(jnp.bfloat16)


def exchange(pieces, axes):
    return lax.all_to_all(pieces, axes, 0, 0, tiled=True)


def total_of(got):
    return jnp.sum(got.astype(jnp.float32), 0)


def fold_kernel(got_ref, copies_ref):
    count, groups = got_ref.shape[:2]
    for g in range(groups):
        total = got_ref[0, g].astype(jnp.float32)
        for k in range(1, count):
            total = total + got_ref[k, g].astype(jnp.float32)
        total = total.astype(jnp.bfloat16)
        for m in range(copies_ref.shape[1]):
            copies_ref[g, m] = total


def fold(got, copies):
    groups, width, batch = got.shape[1:]
    out = pl.pallas_call(
        fold_kernel,
        out_shape=jax.ShapeDtypeStruct((groups, copies, width, batch), jnp.bfloat16),
        in_specs=[VMEM],
        out_specs=VMEM,
        compiler_params=pltpu.CompilerParams(vmem_limit_bytes=LIMIT),
        name="fold",
    )(got)
    return out.reshape(groups * copies, width, batch)


def to_out_blocks(half):
    if R1 == "A":
        return total_of(exchange(fold(exchange(half, OUT)[:, None], 16), CHIP))
    two = exchange(half.reshape((8, 2) + half.shape[1:]), "z")
    return total_of(exchange(fold(two, 16), PLANE))


def to_in_blocks(half):
    if R0 == "A":
        return total_of(exchange(fold(exchange(half, CHIP)[:, None], 16), OUT))
    both = jnp.broadcast_to(half[None], (2,) + half.shape).reshape((32,) + half.shape[1:])
    return total_of(exchange(fold(exchange(both, PLANE)[:, None], 8), "z"))


def load_kernel(slot_ref, tensor_ref, states_ref, projected_ref, cols_ref):
    states = states_ref[...]
    shape = (cols_ref.shape[0], states.shape[1])
    wanted = lax.broadcasted_iota(jnp.int32, shape, 0) + slot_ref[0] * shape[0]
    pick = (lax.broadcasted_iota(jnp.int32, shape, 1) == wanted).astype(jnp.bfloat16)
    along = (((1,), (1,)), ((), ()))
    cols_ref[...] = lax.dot_general(pick, states, along, preferred_element_type=jnp.float32)
    projected_ref[...] = lax.dot_general(
        tensor_ref[...], states, along, preferred_element_type=jnp.float32
    )


def load(flat, states, slot, width):
    height, modes = flat.shape
    count = states.shape[0]
    return pl.pallas_call(
        load_kernel,
        out_shape=(
            jax.ShapeDtypeStruct((height, count), jnp.float32),
            jax.ShapeDtypeStruct((width, count), jnp.float32),
        ),
        in_specs=[SMEM, VMEM, VMEM],
        out_specs=(VMEM, VMEM),
        compiler_params=pltpu.CompilerParams(vmem_limit_bytes=LIMIT),
        name="load",
    )(slot, flat, states)


def step_kernel(has_prev, keep_total, number, order, *refs):
    slot_ref, low_ref, cols_ref, projected_ref, linear_ref, tensor_ref = refs[:6]
    refs = refs[6:]
    if has_prev:
        prev_ref, refs = refs[0], refs[1:]
    keep_ref, send_ref, refs = refs[0], refs[1], refs[2:]
    if keep_total:
        total_ref, refs = refs[0], refs[1:]
    (pair_ref,) = refs
    rows, batch = low_ref.shape
    width = cols_ref.shape[0]
    mine = slice(number * batch, (number + 1) * batch)
    low = low_ref[...]
    low_float = low.astype(jnp.float32)
    cols = cols_ref[:, mine]
    first = jnp.dot(linear_ref[...], low, preferred_element_type=jnp.float32)
    some = 128 // width
    for c in range(rows // some):
        part = low_float[c * some : (c + 1) * some, :]
        spread = jnp.broadcast_to(part[:, None, :], (some, width, batch))
        here = slice(c * 128, (c + 1) * 128)
        pair = (spread * cols[None]).reshape(128, batch)
        pair_ref[:, here] = pair.T.astype(jnp.bfloat16)
        first = first + jnp.sum(spread * projected_ref[here, mine].reshape(some, width, batch), 0)
    slot = slot_ref[0]
    modes = tensor_ref.shape[1]
    each = 256
    pair = pair_ref[...]
    for n in range(modes // each):
        second = jnp.dot(
            pair, tensor_ref[:, n * each : (n + 1) * each], preferred_element_type=jnp.float32
        ).T
        for k in range(0, each // width, 2):
            block = (n * (each // width) + k) // 2
            halves = []
            for half in range(2):
                piece = second[(k + half) * width : (k + half + 1) * width, :]
                piece = piece + jnp.where(slot == 2 * block + half, first, 0.0)
                if has_prev:
                    piece = piece + prev_ref[half, block]
                if keep_total:
                    total_ref[half, block] = piece
                halves.append(piece)
            even = slot % 2 == 0
            keep_ref[order[block]] = jnp.where(even, halves[0], halves[1])
            send_ref[order[block]] = jnp.where(even, halves[1], halves[0]).astype(jnp.bfloat16)


def step(flat, linear_t, projected, number, cols, low, slot, prev, keep_total, order):
    modes = flat.shape[1]
    width, batch = cols.shape[0], low.shape[1]
    full = (2, modes // (2 * width), width, batch)
    args = [slot, low, cols, projected, linear_t, flat]
    if prev is not None:
        args.append(prev)
    shapes = [jax.ShapeDtypeStruct(full[1:], jnp.float32), jax.ShapeDtypeStruct(full[1:], jnp.bfloat16)]
    if keep_total:
        shapes.append(jax.ShapeDtypeStruct(full, jnp.float32))
    return pl.pallas_call(
        functools.partial(step_kernel, prev is not None, keep_total, number, tuple(order)),
        out_shape=shapes,
        in_specs=[SMEM] + [VMEM] * (len(args) - 1),
        out_specs=[VMEM] * len(shapes),
        scratch_shapes=[pltpu.VMEM((batch, flat.shape[0]), jnp.bfloat16)],
        compiler_params=pltpu.CompilerParams(vmem_limit_bytes=LIMIT),
        name="step",
    )(*args)


def per_device(tensor, linear, adjoint_end, states):
    rows, width, modes = tensor.shape
    steps, batch = states.shape[:2]
    slot = jnp.reshape(lax.axis_index(IN), (1,)).astype(jnp.int32)
    own = adjoint_end.T
    lam = start_rows(own)
    flat = tensor.reshape(rows * width, modes)
    projected, cols = load(flat, states.reshape(steps * batch, modes), slot, width)
    order = range(16) if R1 == "A" else [b % 8 * 2 + b // 8 for b in range(16)]
    last = [b % 4 * 4 + b // 4 for b in range(16)]
    total = None
    for number in range(steps - 1, -1, -1):
        low = lax.all_gather(lam.astype(jnp.bfloat16), "core").reshape(rows, batch)
        keep, send, *rest = step(
            flat, linear.T, projected, number, cols, low, slot, total, number > 0, order if number else last
        )
        half = core_half(keep, send)
        if number:
            total = rest[0]
            lam = lam + step_size * to_out_blocks(half)
    return (own + step_size * to_in_blocks(half)).T


def solution(mesh):
    fine = Mesh(mesh.devices.reshape(SIZES), AXES)
    placed = (P(OUT, IN, None), P(OUT, IN), P(None, IN), P())
    return jax.shard_map(
        per_device, mesh=fine, in_specs=placed, out_specs=P(None, IN), check_vma=False
    )
```

```python
import functools

import jax
import jax.numpy as jnp
import numpy as np
from jax import lax
from jax.experimental import pallas as pl
from jax.experimental.pallas import tpu as pltpu
from jax.sharding import Mesh, PartitionSpec as P


step_size = 0.5
VMEM = pl.BlockSpec(memory_space=pltpu.VMEM)
SMEM = pl.BlockSpec(memory_space=pltpu.SMEM)
LIMIT = 16 * 1024 * 1024
AXES = ("yhi", "z", "ylo", "x", "core")
SIZES = (2, 8, 4, 4, 2)
OUT = ("yhi", "z")
IN = ("ylo", "x", "core")
CHIP = ("x", "ylo")
PLANE = ("yhi", "ylo", "x")
R1 = "A"
R0 = "A"


def ring(a, b, n):
    d = abs(a - b) % n
    return min(d, n - d)


def spread_pairs():
    pairs = []
    for o in range(16):
        yhi, z = divmod(o, 8)
        ylo, x = divmod(o, 4)
        hold = [(h, k) for h in range(2) for k in range(8)]
        want = [(a, b) for a in range(4) for b in range(4)]
        cost = np.array(
            [
                [ring(k, z, 8) + ring(h * 4 + ylo, yhi * 4 + a, 8) + ring(x, b, 4) for a, b in want]
                for h, k in hold
            ]
        )
        best = assign(cost)
        for i, j in enumerate(best):
            pairs.append(((hold[i][0] * 8 + hold[i][1]) * 16 + o, o * 16 + want[j][0] * 4 + want[j][1]))
    return pairs


def assign(cost):
    n = len(cost)
    weight = cost.astype(np.int64) ** 4
    row_of = [-1] * n
    high, low = [0] * (n + 1), [0] * (n + 1)
    match = [n] * (n + 1)
    for i in range(n):
        match[n] = i
        col = n
        least = [1 << 60] * (n + 1)
        back = [n] * (n + 1)
        used = [False] * (n + 1)
        while match[col] != n:
            used[col] = True
            row, delta, nxt = match[col], 1 << 60, n
            for j in range(n):
                if not used[j]:
                    reduced = int(weight[row][j]) - high[row] - low[j]
                    if reduced < least[j]:
                        least[j], back[j] = reduced, col
                    if least[j] < delta:
                        delta, nxt = least[j], j
            for j in range(n + 1):
                if used[j]:
                    high[match[j]] += delta
                    low[j] -= delta
                else:
                    least[j] -= delta
            col = nxt
        while col != n:
            prev = back[col]
            match[col] = match[prev]
            col = prev
    for j in range(n):
        row_of[match[j]] = j
    return row_of


def start_rows(own):
    perm = [(2 * a + c, 2 * b + c) for a, b in spread_pairs() for c in range(2)]
    return lax.ppermute(own, AXES, perm)


def join_kernel(slot_ref, keep_ref, both_ref, half_ref):
    even = slot_ref[0] % 2 == 0
    got = jnp.where(even, both_ref[1].astype(jnp.float32), both_ref[0].astype(jnp.float32))
    half_ref[...] = (keep_ref[...] + got).astype(jnp.bfloat16)


def core_half(keep, send, slot):
    both = lax.all_gather(send, "core")
    return pl.pallas_call(
        join_kernel,
        out_shape=jax.ShapeDtypeStruct(keep.shape, jnp.bfloat16),
        in_specs=[SMEM, VMEM, VMEM],
        out_specs=VMEM,
        compiler_params=pltpu.CompilerParams(vmem_limit_bytes=LIMIT),
        name="join",
    )(slot, keep, both)


def exchange(pieces, axes):
    return lax.all_to_all(pieces, axes, 0, 0, tiled=True)


def total_of(got):
    return jnp.sum(got.astype(jnp.float32), 0)


def fold_kernel(got_ref, copies_ref):
    count, groups = got_ref.shape[:2]
    for g in range(groups):
        total = got_ref[0, g].astype(jnp.float32)
        for k in range(1, count):
            total = total + got_ref[k, g].astype(jnp.float32)
        total = total.astype(jnp.bfloat16)
        for m in range(copies_ref.shape[1]):
            copies_ref[g, m] = total


def fold(got, copies):
    groups, width, batch = got.shape[1:]
    out = pl.pallas_call(
        fold_kernel,
        out_shape=jax.ShapeDtypeStruct((groups, copies, width, batch), jnp.bfloat16),
        in_specs=[VMEM],
        out_specs=VMEM,
        compiler_params=pltpu.CompilerParams(vmem_limit_bytes=LIMIT),
        name="fold",
    )(got)
    return out.reshape(groups * copies, width, batch)


def to_out_blocks(half):
    if R1 == "A":
        return total_of(exchange(fold(exchange(half, OUT)[:, None], 16), CHIP))
    two = exchange(half.reshape((8, 2) + half.shape[1:]), "z")
    return total_of(exchange(fold(two, 16), PLANE))


def to_in_blocks(half):
    if R0 == "A":
        return total_of(exchange(fold(exchange(half, CHIP)[:, None], 16), OUT))
    both = jnp.broadcast_to(half[None], (2,) + half.shape).reshape((32,) + half.shape[1:])
    return total_of(exchange(fold(exchange(both, PLANE)[:, None], 8), "z"))


ALONG = (((1,), (1,)), ((), ()))


def split_kernel(slot_ref, tensor_ref, mine_ref, give_ref):
    height = mine_ref.shape[0]
    core = slot_ref[0] % 2
    mine_ref[...] = tensor_ref[pl.ds(pl.multiple_of(core * height, height), height), :]
    give_ref[...] = tensor_ref[pl.ds(pl.multiple_of((1 - core) * height, height), height), :]


def split(flat, slot):
    part = jax.ShapeDtypeStruct((flat.shape[0] // 2, flat.shape[1]), flat.dtype)
    return pl.pallas_call(
        split_kernel,
        out_shape=(part, part),
        in_specs=[SMEM, VMEM],
        out_specs=(VMEM, VMEM),
        compiler_params=pltpu.CompilerParams(vmem_limit_bytes=LIMIT),
        name="split",
    )(slot, flat)


def load_kernel(slot_ref, mine_ref, states_ref, projected_ref, cols_ref):
    states = states_ref[...]
    width = cols_ref.shape[0] // 2
    slot = slot_ref[0]
    shape = (width, states.shape[1])
    for part, place in enumerate((slot, slot + 1 - 2 * (slot % 2))):
        wanted = lax.broadcasted_iota(jnp.int32, shape, 0) + place * width
        pick = (lax.broadcasted_iota(jnp.int32, shape, 1) == wanted).astype(jnp.bfloat16)
        cols_ref[part * width : (part + 1) * width, :] = lax.dot_general(
            pick, states, ALONG, preferred_element_type=jnp.float32
        )
    projected_ref[...] = lax.dot_general(mine_ref[...], states, ALONG, preferred_element_type=jnp.float32)


def load(mine, states, slot, width):
    count = states.shape[0]
    return pl.pallas_call(
        load_kernel,
        out_shape=(
            jax.ShapeDtypeStruct((mine.shape[0], count), jnp.float32),
            jax.ShapeDtypeStruct((2 * width, count), jnp.float32),
        ),
        in_specs=[SMEM, VMEM, VMEM],
        out_specs=(VMEM, VMEM),
        compiler_params=pltpu.CompilerParams(vmem_limit_bytes=LIMIT),
        name="load",
    )(slot, mine, states)


def project_kernel(tensor_ref, states_ref, projected_ref):
    projected_ref[...] = lax.dot_general(
        tensor_ref[...], states_ref[...], ALONG, preferred_element_type=jnp.float32
    )


def project(flat, states):
    return pl.pallas_call(
        project_kernel,
        out_shape=jax.ShapeDtypeStruct((flat.shape[0], states.shape[0]), jnp.float32),
        in_specs=[VMEM, VMEM],
        out_specs=VMEM,
        compiler_params=pltpu.CompilerParams(vmem_limit_bytes=LIMIT),
        name="project",
    )(flat, states)


def step_kernel(has_prev, keep_total, number, order, *refs):
    slot_ref, low_ref, cols_ref, own_ref, other_ref, linear_ref, mine_ref, swapped_ref = refs[:8]
    refs = refs[8:]
    if has_prev:
        prev_ref, refs = refs[0], refs[1:]
    keep_ref, send_ref, refs = refs[0], refs[1], refs[2:]
    if keep_total:
        total_ref, refs = refs[0], refs[1:]
    (pair_ref,) = refs
    rows, batch = low_ref.shape
    width = cols_ref.shape[0] // 2
    height = rows * width
    slot = slot_ref[0]
    even = slot % 2 == 0
    now = slice(number * batch, (number + 1) * batch)
    low = low_ref[...]
    low_float = low.astype(jnp.float32)
    none = jnp.zeros((rows, batch), jnp.float32)
    padded = jnp.concatenate([jnp.where(even, low_float, none), jnp.where(even, none, low_float)], 0)
    lin = jnp.dot(linear_ref[...], padded.astype(jnp.bfloat16), preferred_element_type=jnp.float32)
    lin_first, lin_last = lin[:width, :], lin[width:, :]
    lins = (jnp.where(even, lin_first, lin_last), jnp.where(even, lin_last, lin_first))
    some = 128 // width
    firsts = []
    for part, projected_ref in enumerate((own_ref, other_ref)):
        cols = cols_ref[part * width : (part + 1) * width, now]
        first = lins[part]
        for c in range(rows // some):
            spread = jnp.broadcast_to(
                low_float[c * some : (c + 1) * some, :][:, None, :], (some, width, batch)
            )
            here = slice(c * 128, (c + 1) * 128)
            pair = (spread * cols[None]).reshape(128, batch)
            pair_ref[:, part * height + c * 128 : part * height + (c + 1) * 128] = pair.T.astype(jnp.bfloat16)
            first = first + jnp.sum(spread * projected_ref[here, now].reshape(some, width, batch), 0)
        firsts.append(first)
    extra = (jnp.where(even, firsts[0], firsts[1]), jnp.where(even, firsts[1], firsts[0]))
    modes = mine_ref.shape[1]
    each = 256
    pair_own, pair_other = pair_ref[:, :height], pair_ref[:, height:]
    for n in range(modes // each):
        some_modes = pl.ds(n * each, each)
        second = jnp.dot(
            pair_own, mine_ref[:, some_modes], preferred_element_type=jnp.float32
        )
        second = second + jnp.dot(
            pair_other, swapped_ref[:, some_modes], preferred_element_type=jnp.float32
        )
        second = second.T
        for k in range(0, each // width, 2):
            block = (n * (each // width) + k) // 2
            halves = []
            for half in range(2):
                piece = second[(k + half) * width : (k + half + 1) * width, :]
                piece = piece + jnp.where(slot // 2 == block, extra[half], 0.0)
                if has_prev:
                    piece = piece + prev_ref[half, block]
                if keep_total:
                    total_ref[half, block] = piece
                halves.append(piece)
            keep_ref[order[block]] = jnp.where(even, halves[0], halves[1])
            send_ref[order[block]] = jnp.where(even, halves[1], halves[0]).astype(jnp.bfloat16)


def step(mine, swapped, linears, own, other, number, cols, low, slot, prev, keep_total, order):
    modes = mine.shape[1]
    width, batch = cols.shape[0] // 2, low.shape[1]
    full = (2, modes // (2 * width), width, batch)
    args = [slot, low, cols, own, other, linears, mine, swapped]
    if prev is not None:
        args.append(prev)
    shapes = [jax.ShapeDtypeStruct(full[1:], jnp.float32), jax.ShapeDtypeStruct(full[1:], jnp.bfloat16)]
    if keep_total:
        shapes.append(jax.ShapeDtypeStruct(full, jnp.float32))
    return pl.pallas_call(
        functools.partial(step_kernel, prev is not None, keep_total, number, tuple(order)),
        out_shape=shapes,
        in_specs=[SMEM] + [VMEM] * (len(args) - 1),
        out_specs=[VMEM] * len(shapes),
        scratch_shapes=[pltpu.VMEM((batch, 2 * mine.shape[0]), jnp.bfloat16)],
        compiler_params=pltpu.CompilerParams(vmem_limit_bytes=LIMIT),
        name="step",
    )(*args)


def per_device(tensor, linear, adjoint_end, states):
    rows, width, modes = tensor.shape
    steps, batch = states.shape[:2]
    slot = jnp.reshape(lax.axis_index(IN), (1,)).astype(jnp.int32)
    own = adjoint_end.T
    lam = start_rows(own)
    mine, give = split(tensor.reshape(rows * width, modes), slot)
    swapped = lax.ppermute(give, "core", [(0, 1), (1, 0)])
    both_states = states.reshape(steps * batch, modes)
    projected, cols = load(mine, both_states, slot, width)
    linear, projected = lax.optimization_barrier((linear, projected))
    linears = lax.all_gather(linear.T, "core").reshape(2 * width, rows)
    other = project(swapped, both_states)
    order = range(16) if R1 == "A" else [b % 8 * 2 + b // 8 for b in range(16)]
    last = [b % 4 * 4 + b // 4 for b in range(16)]
    total = None
    for number in range(steps - 1, -1, -1):
        keep, send, *rest = step(
            mine, swapped, linears, projected, other, number, cols, lam.astype(jnp.bfloat16), slot, total,
            number > 0, order if number else last,
        )
        part = core_half(keep, send, slot)
        if number:
            total = rest[0]
            lam = lam + step_size * to_out_blocks(part)
    return (own + step_size * to_in_blocks(part)).T


def solution(mesh):
    fine = Mesh(mesh.devices.reshape(SIZES), AXES)
    placed = (P(OUT, IN, None), P(OUT, IN), P(None, IN), P())

    return jax.shard_map(per_device, mesh=fine, in_specs=placed, out_specs=P(None, IN), check_vma=False)
```

```python
import functools

import jax
import jax.numpy as jnp
import numpy as np
from jax import lax
from jax.experimental import pallas as pl
from jax.experimental.pallas import tpu as pltpu
from jax.sharding import Mesh, PartitionSpec as P


step_size = 0.5
VMEM = pl.BlockSpec(memory_space=pltpu.VMEM)
SMEM = pl.BlockSpec(memory_space=pltpu.SMEM)
LIMIT = 16 * 1024 * 1024
AXES = ("yhi", "z", "ylo", "x", "core")
SIZES = (2, 8, 4, 4, 2)
OUT = ("yhi", "z")
IN = ("ylo", "x", "core")
CHIP = ("x", "ylo")
PLANE = ("yhi", "ylo", "x")
R1 = "A"
R0 = "A"


def ring(a, b, n):
    d = abs(a - b) % n
    return min(d, n - d)


def spread_pairs():
    pairs = []
    for o in range(16):
        yhi, z = divmod(o, 8)
        ylo, x = divmod(o, 4)
        hold = [(h, k) for h in range(2) for k in range(8)]
        want = [(a, b) for a in range(4) for b in range(4)]
        cost = np.array(
            [
                [ring(k, z, 8) + ring(h * 4 + ylo, yhi * 4 + a, 8) + ring(x, b, 4) for a, b in want]
                for h, k in hold
            ]
        )
        best = assign(cost)
        for i, j in enumerate(best):
            pairs.append(((hold[i][0] * 8 + hold[i][1]) * 16 + o, o * 16 + want[j][0] * 4 + want[j][1]))
    return pairs


def assign(cost):
    n = len(cost)
    weight = 32 ** cost.astype(np.int64)
    row_of = [-1] * n
    high, low = [0] * (n + 1), [0] * (n + 1)
    match = [n] * (n + 1)
    for i in range(n):
        match[n] = i
        col = n
        least = [1 << 60] * (n + 1)
        back = [n] * (n + 1)
        used = [False] * (n + 1)
        while match[col] != n:
            used[col] = True
            row, delta, nxt = match[col], 1 << 60, n
            for j in range(n):
                if not used[j]:
                    reduced = int(weight[row][j]) - high[row] - low[j]
                    if reduced < least[j]:
                        least[j], back[j] = reduced, col
                    if least[j] < delta:
                        delta, nxt = least[j], j
            for j in range(n + 1):
                if used[j]:
                    high[match[j]] += delta
                    low[j] -= delta
                else:
                    least[j] -= delta
            col = nxt
        while col != n:
            prev = back[col]
            match[col] = match[prev]
            col = prev
    for j in range(n):
        row_of[match[j]] = j
    return row_of


def start_rows(own):
    perm = [(2 * a + c, 2 * b + c) for a, b in spread_pairs() for c in range(2)]
    return lax.ppermute(own, AXES, perm)


def join_kernel(slot_ref, keep_ref, both_ref, half_ref):
    even = slot_ref[0] % 2 == 0
    got = jnp.where(even, both_ref[1].astype(jnp.float32), both_ref[0].astype(jnp.float32))
    half_ref[...] = (keep_ref[...] + got).astype(jnp.bfloat16)


def core_half(keep, send, slot):
    both = lax.all_gather(send, "core")
    return pl.pallas_call(
        join_kernel,
        out_shape=jax.ShapeDtypeStruct(keep.shape, jnp.bfloat16),
        in_specs=[SMEM, VMEM, VMEM],
        out_specs=VMEM,
        compiler_params=pltpu.CompilerParams(vmem_limit_bytes=LIMIT),
        name="join",
    )(slot, keep, both)


def exchange(pieces, axes):
    return lax.all_to_all(pieces, axes, 0, 0, tiled=True)


def total_of(got):
    return jnp.sum(got.astype(jnp.float32), 0)


def fold_kernel(got_ref, copies_ref):
    count, groups = got_ref.shape[:2]
    for g in range(groups):
        total = got_ref[0, g].astype(jnp.float32)
        for k in range(1, count):
            total = total + got_ref[k, g].astype(jnp.float32)
        total = total.astype(jnp.bfloat16)
        for m in range(copies_ref.shape[1]):
            copies_ref[g, m] = total


def fold(got, copies):
    groups, width, batch = got.shape[1:]
    out = pl.pallas_call(
        fold_kernel,
        out_shape=jax.ShapeDtypeStruct((groups, copies, width, batch), jnp.bfloat16),
        in_specs=[VMEM],
        out_specs=VMEM,
        compiler_params=pltpu.CompilerParams(vmem_limit_bytes=LIMIT),
        name="fold",
    )(got)
    return out.reshape(groups * copies, width, batch)


def to_out_blocks(half):
    if R1 == "A":
        return total_of(exchange(fold(exchange(half, OUT)[:, None], 16), CHIP))
    two = exchange(half.reshape((8, 2) + half.shape[1:]), "z")
    return total_of(exchange(fold(two, 16), PLANE))


def to_in_blocks(half):
    if R0 == "A":
        return total_of(exchange(fold(exchange(half, CHIP)[:, None], 16), OUT))
    both = jnp.broadcast_to(half[None], (2,) + half.shape).reshape((32,) + half.shape[1:])
    return total_of(exchange(fold(exchange(both, PLANE)[:, None], 8), "z"))


ALONG = (((1,), (1,)), ((), ()))


def split_kernel(slot_ref, tensor_ref, linear_ref, mine_ref, give_ref):
    width, rows = linear_ref.shape
    height = tensor_ref.shape[0] // 2
    core = slot_ref[0] % 2
    tail = slice(height, height + width)
    for ref, part in ((mine_ref, core), (give_ref, 1 - core)):
        ref[:height, :] = tensor_ref[pl.ds(pl.multiple_of(part * height, height), height), :]
        ref[tail, :] = jnp.zeros((width, ref.shape[1]), ref.dtype)
        ref[tail, : rows // 2] = jnp.where(
            part == 0, linear_ref[:, : rows // 2].astype(jnp.float32), linear_ref[:, rows // 2 :].astype(jnp.float32)
        ).astype(ref.dtype)


def split(flat, linear_t, slot):
    part = jax.ShapeDtypeStruct((flat.shape[0] // 2 + linear_t.shape[0], flat.shape[1]), flat.dtype)
    return pl.pallas_call(
        split_kernel,
        out_shape=(part, part),
        in_specs=[SMEM, VMEM, VMEM],
        out_specs=(VMEM, VMEM),
        compiler_params=pltpu.CompilerParams(vmem_limit_bytes=LIMIT),
        name="split",
    )(slot, flat, linear_t)


def load_kernel(slot_ref, mine_ref, states_ref, projected_ref, cols_ref):
    states = states_ref[...]
    width = cols_ref.shape[0] // 2
    slot = slot_ref[0]
    shape = (width, states.shape[1])
    for part, place in enumerate((slot, slot + 1 - 2 * (slot % 2))):
        wanted = lax.broadcasted_iota(jnp.int32, shape, 0) + place * width
        pick = (lax.broadcasted_iota(jnp.int32, shape, 1) == wanted).astype(jnp.bfloat16)
        cols_ref[part * width : (part + 1) * width, :] = lax.dot_general(
            pick, states, ALONG, preferred_element_type=jnp.float32
        )
    rows = mine_ref[: projected_ref.shape[0], :]
    projected_ref[...] = lax.dot_general(rows, states, ALONG, preferred_element_type=jnp.float32)


def load(mine, states, slot, width):
    count = states.shape[0]
    return pl.pallas_call(
        load_kernel,
        out_shape=(
            jax.ShapeDtypeStruct((mine.shape[0] - width, count), jnp.float32),
            jax.ShapeDtypeStruct((2 * width, count), jnp.float32),
        ),
        in_specs=[SMEM, VMEM, VMEM],
        out_specs=(VMEM, VMEM),
        compiler_params=pltpu.CompilerParams(vmem_limit_bytes=LIMIT),
        name="load",
    )(slot, mine, states)


def project_kernel(tensor_ref, states_ref, projected_ref):
    rows = tensor_ref[: projected_ref.shape[0], :]
    projected_ref[...] = lax.dot_general(rows, states_ref[...], ALONG, preferred_element_type=jnp.float32)


def project(flat, states, width):
    return pl.pallas_call(
        project_kernel,
        out_shape=jax.ShapeDtypeStruct((flat.shape[0] - width, states.shape[0]), jnp.float32),
        in_specs=[VMEM, VMEM],
        out_specs=VMEM,
        compiler_params=pltpu.CompilerParams(vmem_limit_bytes=LIMIT),
        name="project",
    )(flat, states)


def step_kernel(has_prev, keep_total, number, order, *refs):
    slot_ref, low_ref, cols_ref, own_ref, other_ref, mine_ref, swapped_ref = refs[:7]
    refs = refs[7:]
    if has_prev:
        prev_ref, refs = refs[0], refs[1:]
    keep_ref, send_ref, refs = refs[0], refs[1], refs[2:]
    if keep_total:
        total_ref, refs = refs[0], refs[1:]
    (pair_ref,) = refs
    rows, batch = low_ref.shape
    width = cols_ref.shape[0] // 2
    height = rows * width
    slot = slot_ref[0]
    even = slot % 2 == 0
    now = slice(number * batch, (number + 1) * batch)
    low = low_ref[...]
    low_float = low.astype(jnp.float32)
    tail = slice(height, height + width)
    lins = [
        jnp.dot(ref[tail, :rows], low, preferred_element_type=jnp.float32) for ref in (mine_ref, swapped_ref)
    ]
    some = 128 // width
    firsts = []
    for part, projected_ref in enumerate((own_ref, other_ref)):
        cols = cols_ref[part * width : (part + 1) * width, now]
        first = lins[part]
        for c in range(rows // some):
            spread = jnp.broadcast_to(
                low_float[c * some : (c + 1) * some, :][:, None, :], (some, width, batch)
            )
            here = slice(c * 128, (c + 1) * 128)
            pair = (spread * cols[None]).reshape(128, batch)
            pair_ref[:, part * height + c * 128 : part * height + (c + 1) * 128] = pair.T.astype(jnp.bfloat16)
            first = first + jnp.sum(spread * projected_ref[here, now].reshape(some, width, batch), 0)
        firsts.append(first)
    extra = (jnp.where(even, firsts[0], firsts[1]), jnp.where(even, firsts[1], firsts[0]))
    modes = mine_ref.shape[1]
    each = 256
    pair_own, pair_other = pair_ref[:, :height], pair_ref[:, height:]
    for n in range(modes // each):
        some_modes = pl.ds(n * each, each)
        second = jnp.dot(
            pair_own, mine_ref[:height, some_modes], preferred_element_type=jnp.float32
        )
        second = second + jnp.dot(
            pair_other, swapped_ref[:height, some_modes], preferred_element_type=jnp.float32
        )
        second = second.T
        for k in range(0, each // width, 2):
            block = (n * (each // width) + k) // 2
            halves = []
            for half in range(2):
                piece = second[(k + half) * width : (k + half + 1) * width, :]
                piece = piece + jnp.where(slot // 2 == block, extra[half], 0.0)
                if has_prev:
                    piece = piece + prev_ref[half, block]
                if keep_total:
                    total_ref[half, block] = piece
                halves.append(piece)
            keep_ref[order[block]] = jnp.where(even, halves[0], halves[1])
            send_ref[order[block]] = jnp.where(even, halves[1], halves[0]).astype(jnp.bfloat16)


def step(mine, swapped, own, other, number, cols, low, slot, prev, keep_total, order):
    modes = mine.shape[1]
    width, batch = cols.shape[0] // 2, low.shape[1]
    full = (2, modes // (2 * width), width, batch)
    args = [slot, low, cols, own, other, mine, swapped]
    if prev is not None:
        args.append(prev)
    shapes = [jax.ShapeDtypeStruct(full[1:], jnp.float32), jax.ShapeDtypeStruct(full[1:], jnp.bfloat16)]
    if keep_total:
        shapes.append(jax.ShapeDtypeStruct(full, jnp.float32))
    return pl.pallas_call(
        functools.partial(step_kernel, prev is not None, keep_total, number, tuple(order)),
        out_shape=shapes,
        in_specs=[SMEM] + [VMEM] * (len(args) - 1),
        out_specs=[VMEM] * len(shapes),
        scratch_shapes=[pltpu.VMEM((batch, 2 * own.shape[0]), jnp.bfloat16)],
        compiler_params=pltpu.CompilerParams(vmem_limit_bytes=LIMIT),
        name="step",
    )(*args)


def per_device(tensor, linear, adjoint_end, states):
    rows, width, modes = tensor.shape
    steps, batch = states.shape[:2]
    slot = jnp.reshape(lax.axis_index(IN), (1,)).astype(jnp.int32)
    own = adjoint_end.T
    lam = start_rows(own)
    mine, give = split(tensor.reshape(rows * width, modes), linear.T, slot)
    swapped = lax.ppermute(give, "core", [(0, 1), (1, 0)])
    both_states = states.reshape(steps * batch, modes)
    projected, cols = load(mine, both_states, slot, width)
    other = project(swapped, both_states, width)
    order = range(16) if R1 == "A" else [b % 8 * 2 + b // 8 for b in range(16)]
    last = [b % 4 * 4 + b // 4 for b in range(16)]
    total = None
    for number in range(steps - 1, -1, -1):
        keep, send, *rest = step(
            mine, swapped, projected, other, number, cols, lam.astype(jnp.bfloat16), slot, total,
            number > 0, order if number else last,
        )
        part = core_half(keep, send, slot)
        if number:
            total = rest[0]
            lam = lam + step_size * to_out_blocks(part)
    return (own + step_size * to_in_blocks(part)).T


def solution(mesh):
    fine = Mesh(mesh.devices.reshape(SIZES), AXES)
    placed = (P(OUT, IN, None), P(OUT, IN), P(None, IN), P())

    return jax.shard_map(per_device, mesh=fine, in_specs=placed, out_specs=P(None, IN), check_vma=False)
```

```python
import functools

import jax
import jax.numpy as jnp
import numpy as np
from jax import lax
from jax.experimental import pallas as pl
from jax.experimental.pallas import tpu as pltpu
from jax.sharding import Mesh, PartitionSpec as P


step_size = 0.5
VMEM = pl.BlockSpec(memory_space=pltpu.VMEM)
SMEM = pl.BlockSpec(memory_space=pltpu.SMEM)
LIMIT = 16 * 1024 * 1024
LOAD_LIMIT = 48 * 1024 * 1024
CHUNKS = 4
AXES = ("yhi", "z", "ylo", "x", "core")
SIZES = (2, 8, 4, 4, 2)
OUT = ("yhi", "z")
IN = ("ylo", "x", "core")
CHIP = ("x", "ylo")
PLANE = ("yhi", "ylo", "x")
R1 = "A"
R0 = "A"


def ring(a, b, n):
    d = abs(a - b) % n
    return min(d, n - d)


def spread_pairs():
    pairs = []
    for o in range(16):
        yhi, z = divmod(o, 8)
        ylo, x = divmod(o, 4)
        hold = [(h, k) for h in range(2) for k in range(8)]
        want = [(a, b) for a in range(4) for b in range(4)]
        cost = np.array(
            [
                [ring(k, z, 8) + ring(h * 4 + ylo, yhi * 4 + a, 8) + ring(x, b, 4) for a, b in want]
                for h, k in hold
            ]
        )
        best = assign(cost)
        for i, j in enumerate(best):
            pairs.append(((hold[i][0] * 8 + hold[i][1]) * 16 + o, o * 16 + want[j][0] * 4 + want[j][1]))
    return pairs


def assign(cost):
    n = len(cost)
    weight = cost.astype(np.int64) ** 4
    row_of = [-1] * n
    high, low = [0] * (n + 1), [0] * (n + 1)
    match = [n] * (n + 1)
    for i in range(n):
        match[n] = i
        col = n
        least = [1 << 60] * (n + 1)
        back = [n] * (n + 1)
        used = [False] * (n + 1)
        while match[col] != n:
            used[col] = True
            row, delta, nxt = match[col], 1 << 60, n
            for j in range(n):
                if not used[j]:
                    reduced = int(weight[row][j]) - high[row] - low[j]
                    if reduced < least[j]:
                        least[j], back[j] = reduced, col
                    if least[j] < delta:
                        delta, nxt = least[j], j
            for j in range(n + 1):
                if used[j]:
                    high[match[j]] += delta
                    low[j] -= delta
                else:
                    least[j] -= delta
            col = nxt
        while col != n:
            prev = back[col]
            match[col] = match[prev]
            col = prev
    for j in range(n):
        row_of[match[j]] = j
    return row_of


def start_rows(own):
    perm = [(2 * a + c, 2 * b + c) for a, b in spread_pairs() for c in range(2)]
    return lax.ppermute(own, AXES, perm)


def quadrant(linear_ref, first):
    rows = linear_ref.shape[1] // 2
    left, right = linear_ref[:, :rows].astype(jnp.float32), linear_ref[:, rows:].astype(jnp.float32)
    return jnp.where(first, left, right).astype(jnp.bfloat16)


def join_kernel(has_prev, order, slot_ref, keep_ref, both_ref, linear_ref, *refs):
    half_ref, rest_ref = refs[-2:]
    slot = slot_ref[0]
    even = slot % 2 == 0
    blocks = keep_ref.shape[0]
    low = jnp.where(even, both_ref[1, blocks].astype(jnp.float32), both_ref[0, blocks].astype(jnp.float32))
    rest = jnp.dot(
        quadrant(linear_ref, ~even), low.astype(jnp.bfloat16), preferred_element_type=jnp.float32
    )
    if has_prev:
        rest = rest + refs[0][...]
    rest_ref[...] = rest
    for block in range(blocks):
        at = order[block]
        got = jnp.where(even, both_ref[1, at].astype(jnp.float32), both_ref[0, at].astype(jnp.float32))
        here = jnp.where(slot // 2 == block, rest, 0.0)
        half_ref[at] = (keep_ref[at] + got + here).astype(jnp.bfloat16)


def core_half(keep, send, slot, linear_t, prev, order):
    both = lax.all_gather(send, "core")
    args = [slot, keep, both, linear_t] + ([] if prev is None else [prev])
    return pl.pallas_call(
        functools.partial(join_kernel, prev is not None, tuple(order)),
        out_shape=(
            jax.ShapeDtypeStruct(keep.shape, jnp.bfloat16),
            jax.ShapeDtypeStruct(keep.shape[1:], jnp.float32),
        ),
        in_specs=[SMEM] + [VMEM] * (len(args) - 1),
        out_specs=(VMEM, VMEM),
        compiler_params=pltpu.CompilerParams(vmem_limit_bytes=LIMIT),
        name="join",
    )(*args)


def exchange(pieces, axes):
    return lax.all_to_all(pieces, axes, 0, 0, tiled=True)


def total_of(got):
    return jnp.sum(got.astype(jnp.float32), 0)


def fold_kernel(got_ref, copies_ref):
    count, groups = got_ref.shape[:2]
    for g in range(groups):
        total = got_ref[0, g].astype(jnp.float32)
        for k in range(1, count):
            total = total + got_ref[k, g].astype(jnp.float32)
        total = total.astype(jnp.bfloat16)
        for m in range(copies_ref.shape[1]):
            copies_ref[g, m] = total


def fold(got, copies):
    groups, width, batch = got.shape[1:]
    out = pl.pallas_call(
        fold_kernel,
        out_shape=jax.ShapeDtypeStruct((groups, copies, width, batch), jnp.bfloat16),
        in_specs=[VMEM],
        out_specs=VMEM,
        compiler_params=pltpu.CompilerParams(vmem_limit_bytes=LIMIT),
        name="fold",
    )(got)
    return out.reshape(groups * copies, width, batch)


def to_out_blocks(half):
    if R1 == "A":
        return total_of(exchange(fold(exchange(half, OUT)[:, None], 16), CHIP))
    two = exchange(half.reshape((8, 2) + half.shape[1:]), "z")
    return total_of(exchange(fold(two, 16), PLANE))


def to_in_blocks(half):
    if R0 == "A":
        return total_of(exchange(fold(exchange(half, CHIP)[:, None], 16), OUT))
    both = jnp.broadcast_to(half[None], (2,) + half.shape).reshape((32,) + half.shape[1:])
    return total_of(exchange(fold(exchange(both, PLANE)[:, None], 8), "z"))


ALONG = (((1,), (1,)), ((), ()))


def split_kernel(slot_ref, tensor_ref, give_ref, sem):
    height = give_ref.shape[0]
    start = pl.multiple_of((1 - slot_ref[0] % 2) * height, height)
    copy = pltpu.make_async_copy(tensor_ref.at[pl.ds(start, height)], give_ref, sem)
    copy.start()
    copy.wait()


def split(flat, slot):
    return pl.pallas_call(
        split_kernel,
        out_shape=jax.ShapeDtypeStruct((flat.shape[0] // 2, flat.shape[1]), flat.dtype),
        in_specs=[SMEM, pl.BlockSpec(memory_space=pl.ANY)],
        out_specs=VMEM,
        scratch_shapes=[pltpu.SemaphoreType.DMA],
        compiler_params=pltpu.CompilerParams(vmem_limit_bytes=LOAD_LIMIT),
        name="split",
    )(slot, flat)


def load_kernel(slot_ref, tensor_ref, states_ref, mine_ref, projected_ref, cols_ref, sems):
    slot = slot_ref[0]
    height = mine_ref.shape[0]
    each = height // CHUNKS
    copies = []
    for c in range(CHUNKS):
        start = pl.multiple_of(slot % 2 * height + c * each, each)
        copies.append(
            pltpu.make_async_copy(
                tensor_ref.at[pl.ds(start, each)], mine_ref.at[pl.ds(c * each, each)], sems.at[c]
            )
        )
        copies[-1].start()
    states = states_ref[...]
    width = cols_ref.shape[0] // 2
    shape = (width, states.shape[1])
    for part, place in enumerate((slot, slot + 1 - 2 * (slot % 2))):
        wanted = lax.broadcasted_iota(jnp.int32, shape, 0) + place * width
        pick = (lax.broadcasted_iota(jnp.int32, shape, 1) == wanted).astype(jnp.bfloat16)
        cols_ref[part * width : (part + 1) * width, :] = lax.dot_general(
            pick, states, ALONG, preferred_element_type=jnp.float32
        )
    for c in range(CHUNKS):
        copies[c].wait()
        rows = slice(c * each, (c + 1) * each)
        projected_ref[rows, :] = lax.dot_general(
            mine_ref[rows, :], states, ALONG, preferred_element_type=jnp.float32
        )


def load(flat, states, slot, width):
    count = states.shape[0]
    half = flat.shape[0] // 2
    return pl.pallas_call(
        load_kernel,
        out_shape=(
            jax.ShapeDtypeStruct((half, flat.shape[1]), flat.dtype),
            jax.ShapeDtypeStruct((half, count), jnp.float32),
            jax.ShapeDtypeStruct((2 * width, count), jnp.float32),
        ),
        in_specs=[SMEM, pl.BlockSpec(memory_space=pl.ANY), VMEM],
        out_specs=(VMEM, VMEM, VMEM),
        scratch_shapes=[pltpu.SemaphoreType.DMA((CHUNKS,))],
        compiler_params=pltpu.CompilerParams(vmem_limit_bytes=LOAD_LIMIT),
        name="load",
    )(slot, flat, states)


def project_kernel(tensor_ref, states_ref, projected_ref):
    projected_ref[...] = lax.dot_general(
        tensor_ref[...], states_ref[...], ALONG, preferred_element_type=jnp.float32
    )


def project(flat, states):
    return pl.pallas_call(
        project_kernel,
        out_shape=jax.ShapeDtypeStruct((flat.shape[0], states.shape[0]), jnp.float32),
        in_specs=[VMEM, VMEM],
        out_specs=VMEM,
        compiler_params=pltpu.CompilerParams(vmem_limit_bytes=LIMIT),
        name="project",
    )(flat, states)


def step_kernel(has_prev, keep_total, number, order, *refs):
    slot_ref, low_ref, cols_ref, own_ref, other_ref, linear_ref, mine_ref, swapped_ref = refs[:8]
    refs = refs[8:]
    if has_prev:
        prev_ref, refs = refs[0], refs[1:]
    keep_ref, send_ref, refs = refs[0], refs[1], refs[2:]
    if keep_total:
        total_ref, refs = refs[0], refs[1:]
    (pair_ref,) = refs
    rows, batch = low_ref.shape
    width = cols_ref.shape[0] // 2
    height = rows * width
    slot = slot_ref[0]
    even = slot % 2 == 0
    now = slice(number * batch, (number + 1) * batch)
    low = low_ref[...]
    low_float = low.astype(jnp.float32)
    lin = jnp.dot(quadrant(linear_ref, even), low, preferred_element_type=jnp.float32)
    lins = (lin, jnp.zeros_like(lin))
    some = 128 // width
    firsts = []
    for part, projected_ref in enumerate((own_ref, other_ref)):
        cols = cols_ref[part * width : (part + 1) * width, now]
        first = lins[part]
        for c in range(rows // some):
            spread = jnp.broadcast_to(
                low_float[c * some : (c + 1) * some, :][:, None, :], (some, width, batch)
            )
            here = slice(c * 128, (c + 1) * 128)
            pair = (spread * cols[None]).reshape(128, batch)
            pair_ref[:, part * height + c * 128 : part * height + (c + 1) * 128] = pair.T.astype(jnp.bfloat16)
            first = first + jnp.sum(spread * projected_ref[here, now].reshape(some, width, batch), 0)
        firsts.append(first)
    extra = (jnp.where(even, firsts[0], firsts[1]), jnp.where(even, firsts[1], firsts[0]))
    modes = mine_ref.shape[1]
    each = 256
    pair_own, pair_other = pair_ref[:, :height], pair_ref[:, height:]
    for n in range(modes // each):
        some_modes = pl.ds(n * each, each)
        second = jnp.dot(
            pair_own, mine_ref[:, some_modes], preferred_element_type=jnp.float32
        )
        second = second + jnp.dot(
            pair_other, swapped_ref[:, some_modes], preferred_element_type=jnp.float32
        )
        second = second.T
        for k in range(0, each // width, 2):
            block = (n * (each // width) + k) // 2
            halves = []
            for half in range(2):
                piece = second[(k + half) * width : (k + half + 1) * width, :]
                piece = piece + jnp.where(slot // 2 == block, extra[half], 0.0)
                if has_prev:
                    piece = piece + prev_ref[half, block]
                if keep_total:
                    total_ref[half, block] = piece
                halves.append(piece)
            keep_ref[order[block]] = jnp.where(even, halves[0], halves[1])
            send_ref[order[block]] = jnp.where(even, halves[1], halves[0]).astype(jnp.bfloat16)
    send_ref[keep_ref.shape[0]] = low


def step(mine, swapped, linears, own, other, number, cols, low, slot, prev, keep_total, order):
    modes = mine.shape[1]
    width, batch = cols.shape[0] // 2, low.shape[1]
    full = (2, modes // (2 * width), width, batch)
    args = [slot, low, cols, own, other, linears, mine, swapped]
    if prev is not None:
        args.append(prev)
    shapes = [jax.ShapeDtypeStruct(full[1:], jnp.float32)]
    shapes.append(jax.ShapeDtypeStruct((full[1] + 1,) + full[2:], jnp.bfloat16))
    if keep_total:
        shapes.append(jax.ShapeDtypeStruct(full, jnp.float32))
    return pl.pallas_call(
        functools.partial(step_kernel, prev is not None, keep_total, number, tuple(order)),
        out_shape=shapes,
        in_specs=[SMEM] + [VMEM] * (len(args) - 1),
        out_specs=[VMEM] * len(shapes),
        scratch_shapes=[pltpu.VMEM((batch, 2 * mine.shape[0]), jnp.bfloat16)],
        compiler_params=pltpu.CompilerParams(vmem_limit_bytes=LIMIT),
        name="step",
    )(*args)


def per_device(tensor, linear, adjoint_end, states):
    rows, width, modes = tensor.shape
    steps, batch = states.shape[:2]
    slot = jnp.reshape(lax.axis_index(IN), (1,)).astype(jnp.int32)
    own = adjoint_end.T
    lam = start_rows(own)
    flat = tensor.reshape(rows * width, modes)
    give = split(flat, slot)
    swapped = lax.ppermute(give, "core", [(0, 1), (1, 0)])
    both_states = states.reshape(steps * batch, modes)
    mine, projected, cols = load(flat, both_states, slot, width)
    linear_t = linear.T
    other = project(swapped, both_states)
    order = range(16) if R1 == "A" else [b % 8 * 2 + b // 8 for b in range(16)]
    last = [b % 4 * 4 + b // 4 for b in range(16)]
    total = rest_lin = None
    for number in range(steps - 1, -1, -1):
        keep, send, *rest = step(
            mine, swapped, linear_t, projected, other, number, cols, lam.astype(jnp.bfloat16), slot, total,
            number > 0, order if number else last,
        )
        part, rest_lin = core_half(keep, send, slot, linear_t, rest_lin, order if number else last)
        if number:
            total = rest[0]
            lam = lam + step_size * to_out_blocks(part)
    return (own + step_size * to_in_blocks(part)).T


def solution(mesh):
    fine = Mesh(mesh.devices.reshape(SIZES), AXES)
    placed = (P(OUT, IN, None), P(OUT, IN), P(None, IN), P())

    return jax.shard_map(per_device, mesh=fine, in_specs=placed, out_specs=P(None, IN), check_vma=False)
```
